32 devices in a mesh: grp: 4 (over y, x), slab: 8 (over z, core).
Axes of the slice: x: 2, y: 2, z: 4, core: 2. Of those that a mesh axis runs over, the one named last changes fastest.
Arguments:
- fields: float32 [64, 64, 8, 128], P('grp', 'slab'), may hold values from -6 to 6
- velocity: int32 [3, 64, 8, 128], P(None, 'slab'), may hold values from -2 to 2
- diffusivity: float32 [64, 8, 128], P('slab'), may hold values from 0.005 to 0.04
- sensor_offsets: int32 [49152], P('slab'), may hold values from 0 to 8191
- sensor_counts: int32 [8], P('slab'), may hold values from 1 to 6144, 16384 in all
- observations: float32 [49152], P('slab'), may hold values from -6 to 6
- noise_scale: float32 [49152], P('slab'), may hold values from 2 to 20
- perturbation: float32 [64, 49152], P('grp', 'slab'), may hold values from -6 to 6
Outputs:
- updated: float32 [64, 64, 8, 128], P('grp', 'slab')
The draws below stay inside these ranges and needn't reach their ends.
Inputs may be any that keep to these rules, and one draw needn't show every extreme that they name: `sensor_counts`: the counts sum to 16384 and the largest is exactly 6144. `sensor_offsets`: slots at or past their slab's count are unused.
All inputs are finite; a program needn't handle non-finite values. No bound on the sum of `sensor_counts` on one device may be relied on, other than what follows from the above.
Results may differ from the reference program's by a relative error of at most 0.00011.
Values sent between devices are 32-bit elements; how exact they have to be, the bound alone decides.
A program may use at most 64 MiB of HBM per device.

```python
import math
import jax
import jax.numpy as jnp
import numpy as np
from jax import lax

PX = 128
PY = 8
MEM_DEV = 16
STEPS = 2
SCAP = 6144
CELLS = 8192
NZ = 64
ENS = 64
OBS = 16384
N_SLAB = 8


def set_ends(drawn, own_key, low, high):
    spot = [jax.random.randint(jax.random.fold_in(own_key, axis), (), 0, length) for axis, length in enumerate(drawn.shape)]
    main_axis = drawn.shape.index(max(drawn.shape))
    neighbour = spot[:main_axis] + [(spot[main_axis] + 1) % drawn.shape[main_axis]] + spot[main_axis + 1:]
    return drawn.at[tuple(spot)].set(low).at[tuple(neighbour)].set(high)


def steps_of(key, dims, split, smallest, high):
    factor_of = 1.0
    for position, shards_of in split:
        steps = jax.random.uniform(jax.random.fold_in(jax.random.fold_in(key, 6), position), (shards_of,), jnp.float32, smallest / len(split), high / len(split))
        factor_of = factor_of * jnp.repeat(jnp.exp(steps), dims[position] // shards_of).reshape((-1,) + (1,) * (len(dims) - 1 - position))
    return factor_of


def split_up(count, total, reach, skew):
    loads = [(1 << 20) // math.isqrt(standing ** skew) + 1 for standing in range(2, count + 1)]
    spare, counts = total - reach - (count - 1), [1] * (count - 1)
    while spare > 0:
        candidates = [i for i in range(count - 1) if counts[i] < reach]
        pool, budget = sum([loads[i] for i in candidates]), spare
        for i in candidates:
            addition = min(reach - counts[i], max(1, budget * loads[i] // pool), spare)
            counts[i] = counts[i] + addition
            spare = spare - addition
    return np.array([reach] + counts)


def uneven_parts(stream_key, number_of, total, reach, slope):
    if number_of == 2:
        one = jax.random.randint(stream_key, (), max(1, total - reach), min(reach, total - 1) + 1)
        return jnp.stack([one, total - one])
    lengths = jnp.asarray(split_up(number_of, total, reach, slope), jnp.int32)
    twos = (number_of - 1) // 2
    donor, taker = lengths[1:1 + 2 * twos:2], lengths[2:2 + 2 * twos:2]
    room = jnp.minimum(donor - 1, reach - taker)
    moved = jax.random.randint(jax.random.fold_in(stream_key, 1), (twos,), 0, 1 << 20) % (room + 1)
    lengths = lengths.at[1:1 + 2 * twos:2].set(donor - moved).at[2:2 + 2 * twos:2].set(taker + moved)
    return lengths[jax.random.permutation(jax.random.fold_in(stream_key, 2), number_of)]


def scatter_about(stream_key, extent, spread, bound, split=(), kind=jnp.bfloat16):
    factor_of = steps_of(stream_key, extent, split, -0.22, 0.18) if split else 1.0
    values = jax.random.normal(stream_key, extent, jnp.float32) * spread * factor_of
    return jnp.minimum(jnp.maximum(values, -bound), bound).astype(kind)


def setup_inputs(seed: int = 0) -> dict:
    key_of = jax.random.split(jax.random.key(seed), 9)
    return {
        "fields": scatter_about(key_of[0], (ENS, NZ, PY, PX), 1.0, 6.0, ((0, 4), (1, 8)), jnp.float32),
        "velocity": set_ends(jax.random.randint(key_of[1], (3, NZ, PY, PX), -2, 3), jax.random.fold_in(key_of[1], 1), -2, 2).astype(jnp.int32),
        "diffusivity": jnp.clip(0.005 + 0.035 * jax.random.uniform(key_of[2], (NZ, PY, PX), jnp.float32) ** steps_of(key_of[2], (NZ, PY, PX), ((0, 8),), -0.2, 0.2), 0.005, 0.04),
        "sensor_offsets": set_ends(jax.random.randint(key_of[3], (N_SLAB * SCAP,), 0, CELLS), jax.random.fold_in(key_of[3], 1), 0, CELLS - 1).astype(jnp.int32),
        "sensor_counts": uneven_parts(key_of[4], N_SLAB, OBS, SCAP, 2).astype(jnp.int32),
        "observations": scatter_about(key_of[5], (N_SLAB * SCAP,), 1.0, 6.0, ((0, 8),), jnp.float32),
        "noise_scale": jnp.clip(jnp.exp(math.log(20.0) - 2.3025851 * jax.random.uniform(key_of[6], (N_SLAB * SCAP,), jnp.float32) ** steps_of(key_of[6], (N_SLAB * SCAP,), ((0, 8),), -0.2, 0.2)), 2.0, 20.0),
        "perturbation": scatter_about(key_of[7], (ENS, N_SLAB * SCAP), 1.0, 6.0, ((0, 4), (1, 8)), jnp.float32),
    }


COURANT = 0.12

def upwind(courant, center, lower_side, upper_side):
    return jnp.maximum(courant, 0.0) * (center - lower_side) + jnp.minimum(courant, 0.0) * (upper_side - center)

def advance(extended, courant, diffusivity):
    center = extended[:, 1:-1]
    below = extended[:, :-2]
    above = extended[:, 2:]
    south = jnp.roll(center, 1, axis=2)
    north = jnp.roll(center, -1, axis=2)
    west = jnp.roll(center, 1, axis=3)
    east = jnp.roll(center, -1, axis=3)
    transport = upwind(courant[0], center, below, above) + upwind(courant[1], center, south, north)
    transport = transport + upwind(courant[2], center, west, east)
    laplace = below + above + south + north + west + east - 6.0 * center
    return center - transport + diffusivity * laplace

def solve_weights(gram_matrix, cross_matrix, spread_root):
    order = gram_matrix.shape[0]
    index_row = jnp.arange(order, dtype=jnp.int32)
    system = jnp.eye(order, dtype=jnp.float32) + gram_matrix

    def factor_column(column, lower_factor):
        row_here = lax.dynamic_slice_in_dim(lower_factor, column, 1, 0)[0]
        needed = lax.dynamic_slice_in_dim(system, column, 1, 1)[:, 0]
        needed = needed - jnp.dot(lower_factor, row_here, precision=lax.Precision.HIGHEST, preferred_element_type=jnp.float32)
        pivot = jnp.sqrt(lax.dynamic_slice_in_dim(needed, column, 1, 0)[0])
        values = jnp.where(index_row >= column, needed / pivot, 0.0)
        marker = (index_row == column).astype(jnp.float32)
        return lower_factor + values[:, None] * marker[None, :]
    lower_factor = lax.fori_loop(0, order, factor_column, jnp.zeros((order, order), jnp.float32))

    def forward_row(row, solved):
        factor_row = lax.dynamic_slice_in_dim(lower_factor, row, 1, 0)[0]
        pivot = lax.dynamic_slice_in_dim(factor_row, row, 1, 0)[0]
        given = lax.dynamic_slice_in_dim(cross_matrix, row, 1, 0)[0]
        value = (given - jnp.dot(factor_row, solved, precision=lax.Precision.HIGHEST, preferred_element_type=jnp.float32)) / pivot
        return lax.dynamic_update_slice_in_dim(solved, value[None, :], row, 0)
    middle = lax.fori_loop(0, order, forward_row, jnp.zeros_like(cross_matrix))

    def backward_row(turn, solved):
        row = order - 1 - turn
        factor_col = lax.dynamic_slice_in_dim(lower_factor, row, 1, 1)[:, 0]
        pivot = lax.dynamic_slice_in_dim(factor_col, row, 1, 0)[0]
        given = lax.dynamic_slice_in_dim(middle, row, 1, 0)[0]
        value = (given - jnp.dot(factor_col, solved, precision=lax.Precision.HIGHEST, preferred_element_type=jnp.float32)) / pivot
        return lax.dynamic_update_slice_in_dim(solved, value[None, :], row, 0)
    result = lax.fori_loop(0, order, backward_row, jnp.zeros_like(cross_matrix))
    return result / spread_root

def reference(fields, velocity, diffusivity, sensor_offsets, sensor_counts, observations, noise_scale, perturbation):
    courant = velocity.astype(jnp.float32) * COURANT

    def evolve(block):
        for counter in range(STEPS):
            extended = jnp.pad(block, ((0, 0), (1, 1), (0, 0), (0, 0)))
            block = advance(extended, courant, diffusivity)
        return block
    evolved = lax.map(evolve, fields.reshape(ENS // MEM_DEV, MEM_DEV, NZ, PY, PX))
    flattened = evolved.reshape(ENS, NZ * PY * PX)
    slab_base = (jnp.arange(N_SLAB, dtype=jnp.int32) * CELLS)[:, None]
    cell_index = (slab_base + sensor_offsets.reshape(N_SLAB, SCAP).astype(jnp.int32)).reshape(-1)
    live_mask = (jnp.arange(SCAP, dtype=jnp.int32)[None, :] < sensor_counts[:, None]).reshape(-1).astype(jnp.float32)
    predicted = jnp.take(flattened, cell_index, axis=1)
    scaled = live_mask * predicted / noise_scale
    misfit = live_mask * ((observations - predicted) / noise_scale + perturbation)
    spread_root = math.sqrt(ENS - 1)
    centered = (scaled - lax.optimization_barrier(jnp.sum(scaled, axis=0)) / ENS) / spread_root
    gram_matrix = jnp.dot(centered, centered.T, precision=lax.Precision.HIGHEST, preferred_element_type=jnp.float32)
    cross_matrix = jnp.dot(centered, misfit.T, precision=lax.Precision.HIGHEST, preferred_element_type=jnp.float32)
    weights = solve_weights(gram_matrix, cross_matrix, spread_root)
    increment = jnp.dot(weights.T, flattened, precision=lax.Precision.HIGHEST, preferred_element_type=jnp.float32)
    return (flattened + increment).reshape(ENS, NZ, PY, PX)
```

```python
import functools

import jax
import jax.numpy as jnp
from jax import lax
from jax.experimental import pallas as pl
from jax.experimental.pallas import tpu as pltpu
from jax.sharding import PartitionSpec as P

STEPS = 2
COURANT = 0.12
LANES = 128
BLOCK = 8
MESH = pl.DeviceIdType.MESH
NT = (((1,), (1,)), ((), ()))
TN = (((0,), (0,)), ((), ()))


def split_two(values):
    high = values.astype(jnp.bfloat16).astype(jnp.float32)
    return high, values - high


def scatter_kernel(groups, count_ref, off_ref, obs_ref, noise_ref, pert_ref, v_ref, w_ref, bt, a2):
    members, slots = pert_ref.shape
    width = bt.shape[0]
    high_count = w_ref.shape[1]
    per_group = high_count // groups
    off = off_ref[...]
    low = off % width
    high = off // width
    slot = lax.broadcasted_iota(jnp.int32, (1, slots), 1)
    noise = noise_ref[...]
    inverse = jnp.where(slot < count_ref[0], 1.0 / noise, 0.0)
    rows = lax.broadcasted_iota(jnp.int32, (width, slots), 0)
    bt[...] = jnp.where(rows == low, 1.0, 0.0).astype(jnp.bfloat16)
    one = bt[...]

    value = (obs_ref[...] / noise + pert_ref[...]) * inverse
    first, second = split_two(value)
    both = jnp.concatenate([first, second], axis=0)

    def group(q, carry):
        for k in range(per_group):
            a2[k * 2 * members : (k + 1) * 2 * members, :] = jnp.where(
                high == q * per_group + k, both, 0.0
            ).astype(jnp.bfloat16)
        res = lax.dot_general(a2[...], bt[...], NT, preferred_element_type=jnp.float32)
        for k in range(per_group):
            part = res[2 * k * members : (2 * k + 1) * members] + res[
                (2 * k + 1) * members : (2 * k + 2) * members
            ]
            for i in range(width // LANES):
                v_ref[(q * per_group + k) * (width // LANES) + i] = part[
                    :, i * LANES : (i + 1) * LANES
                ]
        return carry

    lax.fori_loop(0, groups, group, 0)

    weight = inverse * inverse
    high_rows = lax.broadcasted_iota(jnp.int32, (high_count, slots), 0)
    first, second = split_two(jnp.where(high_rows == high, weight, 0.0))
    stacked = jnp.concatenate([first, second], axis=0).astype(jnp.bfloat16)
    res = lax.dot_general(stacked, one, NT, preferred_element_type=jnp.float32)
    total = res[:high_count] + res[high_count:]
    for i in range(width // LANES):
        w_ref[i] = total[:, i * LANES : (i + 1) * LANES]


def scatter_terms(groups, units, counts, offsets, observations, noise, perturbation):
    members, slots = perturbation.shape
    width = 2 * LANES
    high_count = units * LANES // width
    vmem = pl.BlockSpec(memory_space=pltpu.VMEM)
    return pl.pallas_call(
        functools.partial(scatter_kernel, groups),
        out_shape=(
            jax.ShapeDtypeStruct((units, members, LANES), jnp.float32),
            jax.ShapeDtypeStruct((width // LANES, high_count, LANES), jnp.float32),
        ),
        in_specs=[pl.BlockSpec(memory_space=pltpu.SMEM)] + [vmem] * 4,
        out_specs=(vmem, vmem),
        scratch_shapes=[
            pltpu.VMEM((width, slots), jnp.bfloat16),
            pltpu.VMEM((high_count // groups * 2 * members, slots), jnp.bfloat16),
        ],
        compiler_params=pltpu.CompilerParams(vmem_limit_bytes=48 * 1024 * 1024),
        name="scatter_terms",
    )(counts, offsets[None], observations[None], noise[None], perturbation)


def upwind(courant, center, lower_side, upper_side):
    return jnp.maximum(courant, 0.0) * (center - lower_side) + jnp.minimum(courant, 0.0) * (
        upper_side - center
    )


def advance(below, center, above, cz, cy, cx, diffusivity):
    y_size, x_size = center.shape[1:]
    south = pltpu.roll(center, 1, 1)
    north = pltpu.roll(center, y_size - 1, 1)
    west = pltpu.roll(center, 1, 2)
    east = pltpu.roll(center, x_size - 1, 2)
    transport = upwind(cz, center, below, above) + upwind(cy, center, south, north)
    transport = transport + upwind(cx, center, west, east)
    laplace = below + above + south + north + west + east - 6.0 * center
    return center - transport + diffusivity * laplace


def solve_in_place(m_ref):
    order, width = m_ref.shape

    def block(b, carry):
        start = pl.multiple_of(b * BLOCK, BLOCK)
        whole = m_ref[...]
        rows = m_ref[pl.ds(start, BLOCK), :]
        row_id = lax.broadcasted_iota(jnp.int32, (BLOCK, width), 0)
        cols = [jnp.broadcast_to(rows[:, i : i + 1], (BLOCK, width)) for i in range(BLOCK)]
        for j in range(BLOCK):
            inverse = 1.0 / cols[j][j : j + 1, :]
            mine = cols[j]
            here = row_id == j

            def eliminate(t):
                pivot_row = t[j : j + 1, :] * inverse
                return jnp.where(here, pivot_row, t - mine * pivot_row)

            rows = eliminate(rows)
            for i in range(j + 1, BLOCK):
                cols[i] = eliminate(cols[i])
        new = whole
        for j in range(BLOCK):
            new = new - whole[:, j : j + 1] * rows[j : j + 1, :]
        m_ref[...] = pltpu.roll(new, width - BLOCK, 1)
        m_ref[pl.ds(start, BLOCK), :] = pltpu.roll(rows, width - BLOCK, 1)
        return carry

    lax.fori_loop(0, order // BLOCK, block, 0)


def step_kernel(
    groups,
    slabs,
    v_ref,
    w_ref,
    fields_ref,
    vel_ref,
    dif_ref,
    out_ref,
    ext,
    velx,
    difx,
    mid,
    own,
    eq,
    vq,
    xs,
    xc,
    yz,
    part,
    rs,
    rowsum,
    rg,
    total,
    m_ref,
    upd,
    ret,
    halo_send,
    halo_recv,
    gs_sem,
    gr_sem,
    ss_sem,
    sr_sem,
):
    g, s = lax.axis_index("grp"), lax.axis_index("slab")
    members, planes, ys, xsz = fields_ref.shape
    units = planes * ys
    per = units // groups
    order = members * groups
    depth = order // slabs

    barrier = pltpu.get_barrier_semaphore()
    for r in range(1, groups):
        pl.semaphore_signal(
            barrier, inc=1, device_id=(lax.rem(g + r, groups), s), device_id_type=MESH
        )
    for r in range(1, slabs):
        pl.semaphore_signal(
            barrier, inc=1, device_id=(g, lax.rem(s + r, slabs)), device_id_type=MESH
        )
    pl.semaphore_wait(barrier, groups + slabs - 2)

    def halo(sign, k, src, dst):
        return pltpu.make_async_remote_copy(
            src_ref=src,
            dst_ref=dst,
            send_sem=halo_send.at[(sign + 1) // 2, k],
            recv_sem=halo_recv.at[(sign + 1) // 2, k],
            device_id=(g, lax.rem(s + sign + slabs, slabs)),
            device_id_type=MESH,
        )

    last = planes + STEPS
    up = [
        halo(1, 0, fields_ref.at[:, planes - 2 : planes], ext.at[:, 0:2]),
        halo(1, 1, vel_ref.at[:, planes - 1 : planes], velx.at[:, 0:1]),
        halo(1, 2, dif_ref.at[planes - 1 : planes], difx.at[0:1]),
    ]
    down = [
        halo(-1, 0, fields_ref.at[:, 0:2], ext.at[:, last : last + 2]),
        halo(-1, 1, vel_ref.at[:, 0:1], velx.at[:, planes + 1 : planes + 2]),
        halo(-1, 2, dif_ref.at[0:1], difx.at[planes + 1 : planes + 2]),
    ]

    @pl.when(s < slabs - 1)
    def _():
        for copy in up:
            copy.start()

    @pl.when(s > 0)
    def _():
        for copy in down:
            copy.start()

    def grp_copy(phase, r, src, dst):
        return pltpu.make_async_remote_copy(
            src_ref=src,
            dst_ref=dst,
            send_sem=gs_sem.at[phase, r],
            recv_sem=gr_sem.at[phase, r],
            device_id=(lax.rem(g + r, groups), s),
            device_id_type=MESH,
        )

    def slab_copy(phase, r, src, dst):
        return pltpu.make_async_remote_copy(
            src_ref=src,
            dst_ref=dst,
            send_sem=ss_sem.at[phase, r],
            recv_sem=sr_sem.at[phase, r],
            device_id=(g, lax.rem(s + r, slabs)),
            device_id_type=MESH,
        )

    def units_of(r):
        return pl.ds(lax.rem(g + r, groups) * per, per)

    v_copies = [
        grp_copy(0, r, v_ref.at[units_of(r)], vq.at[g]) for r in range(1, groups)
    ]
    for copy in v_copies:
        copy.start()
    vq[g] = v_ref[units_of(0)]

    ext[:, 2:last] = fields_ref[...]
    velx[:, 1 : planes + 1] = vel_ref[...]
    difx[1 : planes + 1] = dif_ref[...]

    @pl.when(s == 0)
    def _():
        ext[:, 0:2] = jnp.zeros((members, 2, ys, xsz), jnp.float32)
        velx[:, 0:1] = jnp.zeros((3, 1, ys, xsz), jnp.int32)
        difx[0:1] = jnp.zeros((1, ys, xsz), jnp.float32)

    @pl.when(s == slabs - 1)
    def _():
        ext[:, last : last + 2] = jnp.zeros((members, 2, ys, xsz), jnp.float32)
        velx[:, planes + 1 : planes + 2] = jnp.zeros((3, 1, ys, xsz), jnp.int32)
        difx[planes + 1 : planes + 2] = jnp.zeros((1, ys, xsz), jnp.float32)

    @pl.when(s > 0)
    def _():
        for copy in up:
            copy.wait_recv()

    @pl.when(s < slabs - 1)
    def _():
        for copy in down:
            copy.wait_recv()

    def coefficients(p):
        courant = [velx[c, p].astype(jnp.float32)[None] * COURANT for c in range(3)]
        return courant + [difx[p][None]]

    def first_step(p, carry):
        mid[:, p] = advance(ext[:, p], ext[:, p + 1], ext[:, p + 2], *coefficients(p))
        return carry

    lax.fori_loop(0, planes + 2, first_step, 0)

    @pl.when(s == 0)
    def _():
        mid[:, 0] = jnp.zeros((members, ys, xsz), jnp.float32)

    @pl.when(s == slabs - 1)
    def _():
        mid[:, planes + 1] = jnp.zeros((members, ys, xsz), jnp.float32)

    def second_step(p, carry):
        res = advance(mid[:, p], mid[:, p + 1], mid[:, p + 2], *coefficients(p + 1))
        own[pl.ds(p * ys, ys)] = jnp.swapaxes(res, 0, 1)
        return carry

    lax.fori_loop(0, planes, second_step, 0)

    e_copies = [grp_copy(1, r, own.at[units_of(r)], eq.at[g]) for r in range(1, groups)]
    for copy in e_copies:
        copy.start()
    eq[g] = own[units_of(0)]
    for copy in v_copies:
        copy.wait_recv()
    for copy in e_copies:
        copy.wait_recv()

    per_row = w_ref.shape[0]
    first_row = g * (per // per_row)
    for u in range(per):
        lanes = slice(u * LANES, (u + 1) * LANES)
        x = jnp.concatenate([eq[q, u] for q in range(groups)], axis=0)
        v = jnp.concatenate([vq[q, u] for q in range(groups)], axis=0)
        w = w_ref[u % per_row, pl.ds(first_row + u // per_row, 1), :]
        centered = x - jnp.sum(x, axis=0, keepdims=True) / order
        xs[:, lanes] = x
        xc[:, lanes] = centered
        yz[0:order, lanes] = centered * w
        yz[order : 2 * order, lanes] = v - x * w
    part[...] = lax.dot_general(
        xc[...],
        yz[...],
        NT,
        precision=lax.Precision.HIGHEST,
        preferred_element_type=jnp.float32,
    ) / (order - 1)

    def rows_of(r):
        return pl.ds(pl.multiple_of(lax.rem(s + r, slabs) * depth, depth), depth)

    rs_copies = [slab_copy(0, r, part.at[rows_of(r)], rs.at[s]) for r in range(1, slabs)]
    for copy in rs_copies:
        copy.start()
    rs[s] = part[rows_of(0), :]
    for copy in rs_copies:
        copy.wait_recv()
    added = rs[0]
    for i in range(1, slabs):
        added = added + rs[i]
    rowsum[...] = added
    rg_copies = [grp_copy(2, r, rowsum, rg.at[g]) for r in range(1, groups)]
    for copy in rg_copies:
        copy.start()
    rg[g] = added
    for copy in rg_copies:
        copy.wait_recv()
    added = rg[0]
    for i in range(1, groups):
        added = added + rg[i]
    total[...] = added
    ag_copies = [slab_copy(1, r, total, m_ref.at[rows_of(0)]) for r in range(1, slabs)]
    for copy in ag_copies:
        copy.start()
    m_ref[rows_of(0), :] = added
    for copy in ag_copies:
        copy.wait_recv()

    shape = m_ref.shape
    diagonal = lax.broadcasted_iota(jnp.int32, shape, 0) == lax.broadcasted_iota(
        jnp.int32, shape, 1
    )
    m_ref[...] = m_ref[...] + jnp.where(diagonal, 1.0, 0.0)
    solve_in_place(m_ref)

    new = xs[...] + lax.dot_general(
        m_ref[:, 0:order],
        xs[...],
        TN,
        precision=lax.Precision.HIGHEST,
        preferred_element_type=jnp.float32,
    )
    for q in range(groups):
        for u in range(per):
            upd[q, u] = new[q * members : (q + 1) * members, u * LANES : (u + 1) * LANES]
    u_copies = [
        grp_copy(3, r, upd.at[lax.rem(g + r, groups)], ret.at[units_of(0)])
        for r in range(1, groups)
    ]
    for copy in u_copies:
        copy.start()
    ret[units_of(0)] = upd[g]
    for copy in u_copies:
        copy.wait_recv()

    def finish(p, carry):
        out_ref[:, p] = jnp.swapaxes(ret[pl.ds(p * ys, ys)], 0, 1)
        return carry

    lax.fori_loop(0, planes, finish, 0)

    for copy in v_copies + e_copies + rs_copies + rg_copies + ag_copies + u_copies:
        copy.wait_send()

    @pl.when(s < slabs - 1)
    def _():
        for copy in up:
            copy.wait_send()

    @pl.when(s > 0)
    def _():
        for copy in down:
            copy.wait_send()


def local(
    groups,
    slabs,
    fields,
    velocity,
    diffusivity,
    sensor_offsets,
    sensor_counts,
    observations,
    noise_scale,
    perturbation,
):
    members, planes, ys, xsz = fields.shape
    units = planes * ys
    per = units // groups
    order = members * groups
    depth = order // slabs
    terms, weight = scatter_terms(
        groups, units, sensor_counts, sensor_offsets, observations, noise_scale, perturbation
    )
    vmem = pl.BlockSpec(memory_space=pltpu.VMEM)
    f32 = jnp.float32
    scratch = [
        pltpu.VMEM((members, planes + 4, ys, xsz), f32),
        pltpu.VMEM((3, planes + 2, ys, xsz), jnp.int32),
        pltpu.VMEM((planes + 2, ys, xsz), f32),
        pltpu.VMEM((members, planes + 2, ys, xsz), f32),
        pltpu.VMEM((units, members, xsz), f32),
        pltpu.VMEM((groups, per, members, xsz), f32),
        pltpu.VMEM((groups, per, members, xsz), f32),
        pltpu.VMEM((order, per * xsz), f32),
        pltpu.VMEM((order, per * xsz), f32),
        pltpu.VMEM((2 * order, per * xsz), f32),
        pltpu.VMEM((order, 2 * order), f32),
        pltpu.VMEM((slabs, depth, 2 * order), f32),
        pltpu.VMEM((depth, 2 * order), f32),
        pltpu.VMEM((groups, depth, 2 * order), f32),
        pltpu.VMEM((depth, 2 * order), f32),
        pltpu.VMEM((order, 2 * order), f32),
        pltpu.VMEM((groups, per, members, xsz), f32),
        pltpu.VMEM((units, members, xsz), f32),
        pltpu.SemaphoreType.DMA((2, 3)),
        pltpu.SemaphoreType.DMA((2, 3)),
        pltpu.SemaphoreType.DMA((4, groups)),
        pltpu.SemaphoreType.DMA((4, groups)),
        pltpu.SemaphoreType.DMA((2, slabs)),
        pltpu.SemaphoreType.DMA((2, slabs)),
    ]
    return pl.pallas_call(
        functools.partial(step_kernel, groups, slabs),
        out_shape=jax.ShapeDtypeStruct(fields.shape, f32),
        in_specs=[vmem] * 5,
        out_specs=vmem,
        scratch_shapes=scratch,
        compiler_params=pltpu.CompilerParams(
            collective_id=0, has_side_effects=True, vmem_limit_bytes=56 * 1024 * 1024
        ),
        name="ensemble_step",
    )(terms, weight, fields, velocity, diffusivity)


def solution(mesh):
    return jax.shard_map(
        functools.partial(local, mesh.shape["grp"], mesh.shape["slab"]),
        mesh=mesh,
        in_specs=(
            P("grp", "slab", None, None),
            P(None, "slab", None, None),
            P("slab", None, None),
            P("slab"),
            P("slab"),
            P("slab"),
            P("slab"),
            P("grp", "slab"),
        ),
        out_specs=P("grp", "slab", None, None),
        check_vma=False,
    )
```

```python
import functools

import jax
import jax.numpy as jnp
from jax import lax
from jax.experimental import pallas as pl
from jax.experimental.pallas import tpu as pltpu
from jax.sharding import PartitionSpec as P

STEPS = 2
COURANT = 0.12
EARLY = 3
LANES = 128
BLOCK = 8
MESH = pl.DeviceIdType.MESH
NT = (((1,), (1,)), ((), ()))
TN = (((0,), (0,)), ((), ()))


def split_two(values):
    high = values.astype(jnp.bfloat16).astype(jnp.float32)
    return high, values - high


def spread_low(bt, off):
    rows = lax.broadcasted_iota(jnp.int32, bt.shape, 0)
    bt[...] = jnp.where(rows == off % bt.shape[0], 1.0, 0.0).astype(jnp.bfloat16)


def scatter_group(q, high, both, bt, a2, store):
    members = both.shape[0] // 2
    per_group = a2.shape[0] // (2 * members)
    ratio = bt.shape[0] // LANES
    for k in range(per_group):
        a2[k * 2 * members : (k + 1) * 2 * members, :] = jnp.where(
            high[...] == q * per_group + k, both[...], 0.0
        ).astype(jnp.bfloat16)
    res = lax.dot_general(a2[...], bt[...], NT, preferred_element_type=jnp.float32)
    for k in range(per_group):
        start = 2 * k * members
        added = res[start : start + members] + res[start + members : start + 2 * members]
        for i in range(ratio):
            store(k * ratio + i, added[:, i * LANES : (i + 1) * LANES])


def scatter_weights(g, per_group, high, weight, bt, w_ref):
    rows = w_ref.shape[1]
    wanted = lax.broadcasted_iota(jnp.int32, (rows, high.shape[1]), 0) + g * per_group
    first, second = split_two(jnp.where(wanted == high[...], weight, 0.0))
    stacked = jnp.concatenate([first, second], axis=0).astype(jnp.bfloat16)
    res = lax.dot_general(stacked, bt[...], NT, preferred_element_type=jnp.float32)
    total = res[:rows] + res[rows:]
    for i in range(w_ref.shape[0]):
        w_ref[i] = total[:, i * LANES : (i + 1) * LANES]


def upwind(courant, center, lower_side, upper_side):
    return jnp.maximum(courant, 0.0) * (center - lower_side) + jnp.minimum(courant, 0.0) * (
        upper_side - center
    )


def advance(below, center, above, cz, cy, cx, diffusivity):
    y_size, x_size = center.shape[1:]
    south = pltpu.roll(center, 1, 1)
    north = pltpu.roll(center, y_size - 1, 1)
    west = pltpu.roll(center, 1, 2)
    east = pltpu.roll(center, x_size - 1, 2)
    transport = upwind(cz, center, below, above) + upwind(cy, center, south, north)
    transport = transport + upwind(cx, center, west, east)
    laplace = below + above + south + north + west + east - 6.0 * center
    return center - transport + diffusivity * laplace


def solve_in_place(m_ref):
    order, width = m_ref.shape

    def block(b, carry):
        start = pl.multiple_of(b * BLOCK, BLOCK)
        whole = m_ref[...]
        rows = m_ref[pl.ds(start, BLOCK), :]
        row_id = lax.broadcasted_iota(jnp.int32, (BLOCK, width), 0)
        cols = [jnp.broadcast_to(rows[:, i : i + 1], (BLOCK, width)) for i in range(BLOCK)]
        for j in range(BLOCK):
            inverse = 1.0 / cols[j][j : j + 1, :]
            mine = cols[j]
            here = row_id == j

            def eliminate(t):
                pivot_row = t[j : j + 1, :] * inverse
                return jnp.where(here, pivot_row, t - mine * pivot_row)

            rows = eliminate(rows)
            for i in range(j + 1, BLOCK):
                cols[i] = eliminate(cols[i])
        new = whole
        for j in range(BLOCK):
            new = new - whole[:, j : j + 1] * rows[j : j + 1, :]
        m_ref[...] = pltpu.roll(new, width - BLOCK, 1)
        m_ref[pl.ds(start, BLOCK), :] = pltpu.roll(rows, width - BLOCK, 1)
        return carry

    lax.fori_loop(0, order // BLOCK, block, 0)


def step_kernel(
    groups,
    slabs,
    count_ref,
    off_hbm,
    obs_hbm,
    noise_hbm,
    pert_hbm,
    fields_ref,
    vel_ref,
    dif_ref,
    ret,
    off_ref,
    obs_ref,
    noise_ref,
    pert_ref,
    bt,
    a2,
    both,
    v_ref,
    w_ref,
    ext,
    velx,
    difx,
    mid,
    own,
    eq,
    vq,
    xs,
    xc,
    yz,
    part,
    rs,
    rowsum,
    rg,
    total,
    m_ref,
    upd,
    local_sem,
    halo_send,
    halo_recv,
    gs_sem,
    gr_sem,
    ss_sem,
    sr_sem,
):
    g, s = lax.axis_index("grp"), lax.axis_index("slab")
    members, planes, ys, xsz = fields_ref.shape
    units = planes * ys
    per = units // groups
    order = members * groups
    depth = order // slabs
    last = planes + STEPS

    loads = [
        pltpu.make_async_copy(source, target, local_sem.at[i])
        for i, (source, target) in enumerate(
            (
                (off_hbm, off_ref),
                (noise_hbm, noise_ref),
                (obs_hbm, obs_ref),
                (pert_hbm, pert_ref),
                (fields_ref, ext.at[:, 2:last]),
                (vel_ref, velx.at[:, 1 : planes + 1]),
                (dif_ref, difx.at[1 : planes + 1]),
            )
        )
    ]
    for copy in loads:
        copy.start()

    barrier = pltpu.get_barrier_semaphore()
    for r in range(1, groups):
        pl.semaphore_signal(
            barrier, inc=1, device_id=(lax.rem(g + r, groups), s), device_id_type=MESH
        )
    for r in range(1, slabs):
        pl.semaphore_signal(
            barrier, inc=1, device_id=(g, lax.rem(s + r, slabs)), device_id_type=MESH
        )
    loads[0].wait()
    spread_low(bt, off_ref[...])
    pl.semaphore_wait(barrier, groups + slabs - 2)

    def halo(sign, k, src, dst):
        return pltpu.make_async_remote_copy(
            src_ref=src,
            dst_ref=dst,
            send_sem=halo_send.at[(sign + 1) // 2, k],
            recv_sem=halo_recv.at[(sign + 1) // 2, k],
            device_id=(g, lax.rem(s + sign + slabs, slabs)),
            device_id_type=MESH,
        )

    up = [
        halo(1, 0, fields_ref.at[:, planes - 2 : planes], ext.at[:, 0:2]),
        halo(1, 1, vel_ref.at[:, planes - 1 : planes], velx.at[:, 0:1]),
        halo(1, 2, dif_ref.at[planes - 1 : planes], difx.at[0:1]),
    ]
    down = [
        halo(-1, 0, fields_ref.at[:, 0:2], ext.at[:, last : last + 2]),
        halo(-1, 1, vel_ref.at[:, 0:1], velx.at[:, planes + 1 : planes + 2]),
        halo(-1, 2, dif_ref.at[0:1], difx.at[planes + 1 : planes + 2]),
    ]

    @pl.when(s < slabs - 1)
    def _():
        for copy in up:
            copy.start()

    @pl.when(s > 0)
    def _():
        for copy in down:
            copy.start()

    def grp_copy(phase, r, src, dst):
        return pltpu.make_async_remote_copy(
            src_ref=src,
            dst_ref=dst,
            send_sem=gs_sem.at[phase, r],
            recv_sem=gr_sem.at[phase, r],
            device_id=(lax.rem(g + r, groups), s),
            device_id_type=MESH,
        )

    def slab_copy(phase, r, src, dst):
        return pltpu.make_async_remote_copy(
            src_ref=src,
            dst_ref=dst,
            send_sem=ss_sem.at[phase, r],
            recv_sem=sr_sem.at[phase, r],
            device_id=(g, lax.rem(s + r, slabs)),
            device_id_type=MESH,
        )

    def units_of(r):
        return pl.ds(lax.rem(g + r, groups) * per, per)

    for copy in loads[1:4]:
        copy.wait()
    noise = noise_ref[...]
    slot = lax.broadcasted_iota(jnp.int32, noise.shape, 1)
    inverse = jnp.where(slot < count_ref[0], 1.0 / noise, 0.0)
    first, second = split_two((obs_ref[...] / noise + pert_ref[...]) * inverse)
    both[0:members, :] = first
    both[members : 2 * members, :] = second
    off_ref[...] = off_ref[...] // bt.shape[0]

    def v_copy(r):
        return grp_copy(0, r, v_ref.at[units_of(r)], vq.at[g])

    def scatter_turn(r, carry):
        q = lax.rem(g + r, groups)

        def store(u, value):
            v_ref[q * per + u] = value

        scatter_group(q, off_ref, both, bt, a2, store)

        @pl.when(r < groups)
        def _():
            v_copy(r).start()

        return carry

    lax.fori_loop(1, EARLY, scatter_turn, 0)

    for copy in loads[4:]:
        copy.wait()

    @pl.when(s == 0)
    def _():
        ext[:, 0:2] = jnp.zeros((members, 2, ys, xsz), jnp.float32)
        velx[:, 0:1] = jnp.zeros((3, 1, ys, xsz), jnp.int32)
        difx[0:1] = jnp.zeros((1, ys, xsz), jnp.float32)

    @pl.when(s == slabs - 1)
    def _():
        ext[:, last : last + 2] = jnp.zeros((members, 2, ys, xsz), jnp.float32)
        velx[:, planes + 1 : planes + 2] = jnp.zeros((3, 1, ys, xsz), jnp.int32)
        difx[planes + 1 : planes + 2] = jnp.zeros((1, ys, xsz), jnp.float32)

    @pl.when(s > 0)
    def _():
        for copy in up:
            copy.wait_recv()

    @pl.when(s < slabs - 1)
    def _():
        for copy in down:
            copy.wait_recv()

    def coefficients(p):
        courant = [velx[c, p].astype(jnp.float32)[None] * COURANT for c in range(3)]
        return courant + [difx[p][None]]

    def first_step(p, carry):
        mid[:, p] = advance(ext[:, p], ext[:, p + 1], ext[:, p + 2], *coefficients(p))
        return carry

    lax.fori_loop(0, planes + 2, first_step, 0)

    @pl.when(s == 0)
    def _():
        mid[:, 0] = jnp.zeros((members, ys, xsz), jnp.float32)

    @pl.when(s == slabs - 1)
    def _():
        mid[:, planes + 1] = jnp.zeros((members, ys, xsz), jnp.float32)

    def second_step(p, carry):
        res = advance(mid[:, p], mid[:, p + 1], mid[:, p + 2], *coefficients(p + 1))
        own[pl.ds(p * ys, ys)] = jnp.swapaxes(res, 0, 1)
        return carry

    lax.fori_loop(0, planes, second_step, 0)

    e_copies = [grp_copy(1, r, own.at[units_of(r)], eq.at[g]) for r in range(1, groups)]
    for copy in e_copies:
        copy.start()
    eq[g] = own[units_of(0)]
    lax.fori_loop(EARLY, groups + 1, scatter_turn, 0)
    vq[g] = v_ref[units_of(0)]
    scatter_weights(g, per // (bt.shape[0] // LANES), off_ref, inverse * inverse, bt, w_ref)
    v_copies = [v_copy(r) for r in range(1, groups)]
    for copy in v_copies:
        copy.wait_recv()
    for copy in e_copies:
        copy.wait_recv()

    per_row = w_ref.shape[0]
    for u in range(per):
        lanes = slice(u * LANES, (u + 1) * LANES)
        x = jnp.concatenate([eq[q, u] for q in range(groups)], axis=0)
        v = jnp.concatenate([vq[q, u] for q in range(groups)], axis=0)
        w = w_ref[u % per_row, u // per_row : u // per_row + 1, :]
        centered = x - jnp.sum(x, axis=0, keepdims=True) / order
        xs[:, lanes] = x
        xc[:, lanes] = centered
        yz[0:order, lanes] = centered * w
        yz[order : 2 * order, lanes] = v - x * w
    part[...] = lax.dot_general(
        xc[...],
        yz[...],
        NT,
        precision=lax.Precision.HIGHEST,
        preferred_element_type=jnp.float32,
    ) / (order - 1)

    def rows_of(r):
        return pl.ds(pl.multiple_of(lax.rem(s + r, slabs) * depth, depth), depth)

    rs_copies = [slab_copy(0, r, part.at[rows_of(r)], rs.at[s]) for r in range(1, slabs)]
    for copy in rs_copies:
        copy.start()
    rs[s] = part[rows_of(0), :]
    for copy in rs_copies:
        copy.wait_recv()
    added = rs[0]
    for i in range(1, slabs):
        added = added + rs[i]
    rowsum[...] = added
    rg_copies = [grp_copy(2, r, rowsum, rg.at[g]) for r in range(1, groups)]
    for copy in rg_copies:
        copy.start()
    rg[g] = added
    for copy in rg_copies:
        copy.wait_recv()
    added = rg[0]
    for i in range(1, groups):
        added = added + rg[i]
    total[...] = added
    ag_copies = [slab_copy(1, r, total, m_ref.at[rows_of(0)]) for r in range(1, slabs)]
    for copy in ag_copies:
        copy.start()
    m_ref[rows_of(0), :] = added
    for copy in ag_copies:
        copy.wait_recv()

    shape = m_ref.shape
    diagonal = lax.broadcasted_iota(jnp.int32, shape, 0) == lax.broadcasted_iota(
        jnp.int32, shape, 1
    )
    m_ref[...] = m_ref[...] + jnp.where(diagonal, 1.0, 0.0)
    solve_in_place(m_ref)

    new = xs[...] + lax.dot_general(
        m_ref[:, 0:order],
        xs[...],
        TN,
        precision=lax.Precision.HIGHEST,
        preferred_element_type=jnp.float32,
    )
    for q in range(groups):
        for u in range(per):
            upd[q, u] = new[q * members : (q + 1) * members, u * LANES : (u + 1) * LANES]
    u_copies = [
        grp_copy(3, r, upd.at[lax.rem(g + r, groups)], ret.at[units_of(0)])
        for r in range(1, groups)
    ]
    for copy in u_copies:
        copy.start()
    ret[units_of(0)] = upd[g]
    for copy in u_copies:
        copy.wait_recv()

    for copy in v_copies + e_copies + rs_copies + rg_copies + ag_copies + u_copies:
        copy.wait_send()

    @pl.when(s < slabs - 1)
    def _():
        for copy in up:
            copy.wait_send()

    @pl.when(s > 0)
    def _():
        for copy in down:
            copy.wait_send()


def finish_kernel(ret, out_hbm, stage, sem):
    planes = out_hbm.shape[1]
    ys = out_hbm.shape[2]
    copies = []
    for p in range(planes):
        stage[p] = jnp.swapaxes(ret[p * ys : (p + 1) * ys], 0, 1)
        copies.append(pltpu.make_async_copy(stage.at[p], out_hbm.at[:, p], sem.at[p]))
        copies[-1].start()
    for copy in copies:
        copy.wait()


def local(
    groups,
    slabs,
    fields,
    velocity,
    diffusivity,
    sensor_offsets,
    sensor_counts,
    observations,
    noise_scale,
    perturbation,
):
    members, planes, ys, xsz = fields.shape
    units = planes * ys
    per = units // groups
    order = members * groups
    depth = order // slabs
    slots = sensor_offsets.shape[0]
    width = 2 * LANES
    per_group = per * LANES // width
    vmem = pl.BlockSpec(memory_space=pltpu.VMEM)
    f32 = jnp.float32
    scratch = [
        pltpu.VMEM((1, slots), jnp.int32),
        pltpu.VMEM((1, slots), f32),
        pltpu.VMEM((1, slots), f32),
        pltpu.VMEM((members, slots), f32),
        pltpu.VMEM((width, slots), jnp.bfloat16),
        pltpu.VMEM((per_group * 2 * members, slots), jnp.bfloat16),
        pltpu.VMEM((2 * members, slots), f32),
        pltpu.VMEM((units, members, xsz), f32),
        pltpu.VMEM((width // LANES, -(-per_group // 8) * 8, LANES), f32),
        pltpu.VMEM((members, planes + 4, ys, xsz), f32),
        pltpu.VMEM((3, planes + 2, ys, xsz), jnp.int32),
        pltpu.VMEM((planes + 2, ys, xsz), f32),
        pltpu.VMEM((members, planes + 2, ys, xsz), f32),
        pltpu.VMEM((units, members, xsz), f32),
        pltpu.VMEM((groups, per, members, xsz), f32),
        pltpu.VMEM((groups, per, members, xsz), f32),
        pltpu.VMEM((order, per * xsz), f32),
        pltpu.VMEM((order, per * xsz), f32),
        pltpu.VMEM((2 * order, per * xsz), f32),
        pltpu.VMEM((order, 2 * order), f32),
        pltpu.VMEM((slabs, depth, 2 * order), f32),
        pltpu.VMEM((depth, 2 * order), f32),
        pltpu.VMEM((groups, depth, 2 * order), f32),
        pltpu.VMEM((depth, 2 * order), f32),
        pltpu.VMEM((order, 2 * order), f32),
        pltpu.VMEM((groups, per, members, xsz), f32),
        pltpu.SemaphoreType.DMA((7,)),
        pltpu.SemaphoreType.DMA((2, 3)),
        pltpu.SemaphoreType.DMA((2, 3)),
        pltpu.SemaphoreType.DMA((4, groups)),
        pltpu.SemaphoreType.DMA((4, groups)),
        pltpu.SemaphoreType.DMA((2, slabs)),
        pltpu.SemaphoreType.DMA((2, slabs)),
    ]
    anywhere = pl.BlockSpec(memory_space=pl.ANY)
    ret = pl.pallas_call(
        functools.partial(step_kernel, groups, slabs),
        out_shape=jax.ShapeDtypeStruct((units, members, xsz), f32),
        in_specs=[pl.BlockSpec(memory_space=pltpu.SMEM)] + [anywhere] * 7,
        out_specs=vmem,
        scratch_shapes=scratch,
        compiler_params=pltpu.CompilerParams(
            collective_id=0, has_side_effects=True, vmem_limit_bytes=56 * 1024 * 1024
        ),
        name="ensemble_step",
    )(
        sensor_counts,
        sensor_offsets[None],
        observations[None],
        noise_scale[None],
        perturbation,
        fields,
        velocity,
        diffusivity,
    )
    return pl.pallas_call(
        finish_kernel,
        out_shape=jax.ShapeDtypeStruct(fields.shape, f32),
        in_specs=[vmem],
        out_specs=anywhere,
        scratch_shapes=[
            pltpu.VMEM((planes, members, ys, xsz), f32),
            pltpu.SemaphoreType.DMA((planes,)),
        ],
        name="finish",
    )(ret)


def solution(mesh):
    return jax.shard_map(
        functools.partial(local, mesh.shape["grp"], mesh.shape["slab"]),
        mesh=mesh,
        in_specs=(
            P("grp", "slab", None, None),
            P(None, "slab", None, None),
            P("slab", None, None),
            P("slab"),
            P("slab"),
            P("slab"),
            P("slab"),
            P("grp", "slab"),
        ),
        out_specs=P("grp", "slab", None, None),
        check_vma=False,
    )
```

```python
import functools

import jax
import jax.numpy as jnp
from jax import lax
from jax.experimental import pallas as pl
from jax.experimental.pallas import tpu as pltpu
from jax.sharding import PartitionSpec as P

STEPS = 2
COURANT = 0.12
EARLY = 2
LANES = 128
BLOCK = 8
MESH = pl.DeviceIdType.MESH
NT = (((1,), (1,)), ((), ()))
TN = (((0,), (0,)), ((), ()))


def split_two(values):
    high = values.astype(jnp.bfloat16).astype(jnp.float32)
    return high, values - high


def spread_low(bt, off):
    rows = lax.broadcasted_iota(jnp.int32, bt.shape, 0)
    bt[...] = jnp.where(rows == off % bt.shape[0], 1.0, 0.0).astype(jnp.bfloat16)


def scatter_group(q, high, both, bt, a2, store):
    members = both.shape[0] // 2
    per_group = a2.shape[0] // (2 * members)
    ratio = bt.shape[0] // LANES
    for k in range(per_group):
        a2[k * 2 * members : (k + 1) * 2 * members, :] = jnp.where(
            high[...] == q * per_group + k, both[...], 0.0
        ).astype(jnp.bfloat16)
    res = lax.dot_general(a2[...], bt[...], NT, preferred_element_type=jnp.float32)
    for k in range(per_group):
        start = 2 * k * members
        added = res[start : start + members] + res[start + members : start + 2 * members]
        for i in range(ratio):
            store(k * ratio + i, added[:, i * LANES : (i + 1) * LANES])


def scatter_weights(g, per_group, high, weight, bt, w_ref):
    rows = w_ref.shape[1]
    wanted = lax.broadcasted_iota(jnp.int32, (rows, high.shape[1]), 0) + g * per_group
    first, second = split_two(jnp.where(wanted == high[...], weight, 0.0))
    stacked = jnp.concatenate([first, second], axis=0).astype(jnp.bfloat16)
    res = lax.dot_general(stacked, bt[...], NT, preferred_element_type=jnp.float32)
    total = res[:rows] + res[rows:]
    for i in range(w_ref.shape[0]):
        w_ref[i] = total[:, i * LANES : (i + 1) * LANES]


def upwind(courant, center, lower_side, upper_side):
    return jnp.maximum(courant, 0.0) * (center - lower_side) + jnp.minimum(courant, 0.0) * (
        upper_side - center
    )


def advance(below, center, above, cz, cy, cx, diffusivity):
    y_size, x_size = center.shape[1:]
    south = pltpu.roll(center, 1, 1)
    north = pltpu.roll(center, y_size - 1, 1)
    west = pltpu.roll(center, 1, 2)
    east = pltpu.roll(center, x_size - 1, 2)
    transport = upwind(cz, center, below, above) + upwind(cy, center, south, north)
    transport = transport + upwind(cx, center, west, east)
    laplace = below + above + south + north + west + east - 6.0 * center
    return center - transport + diffusivity * laplace


def solve_in_place(m_ref):
    order, width = m_ref.shape

    def block(b, carry):
        start = pl.multiple_of(b * BLOCK, BLOCK)
        whole = m_ref[...]
        rows = m_ref[pl.ds(start, BLOCK), :]
        row_id = lax.broadcasted_iota(jnp.int32, (BLOCK, width), 0)
        cols = [jnp.broadcast_to(rows[:, i : i + 1], (BLOCK, width)) for i in range(BLOCK)]
        for j in range(BLOCK):
            inverse = 1.0 / cols[j][j : j + 1, :]
            mine = cols[j]
            here = row_id == j

            def eliminate(t):
                pivot_row = t[j : j + 1, :] * inverse
                return jnp.where(here, pivot_row, t - mine * pivot_row)

            rows = eliminate(rows)
            for i in range(j + 1, BLOCK):
                cols[i] = eliminate(cols[i])
        new = whole
        for j in range(BLOCK):
            new = new - whole[:, j : j + 1] * rows[j : j + 1, :]
        m_ref[...] = pltpu.roll(new, width - BLOCK, 1)
        m_ref[pl.ds(start, BLOCK), :] = pltpu.roll(rows, width - BLOCK, 1)
        return carry

    lax.fori_loop(0, order // BLOCK, block, 0)


def step_kernel(
    groups,
    slabs,
    count_ref,
    off_hbm,
    obs_hbm,
    noise_hbm,
    pert_hbm,
    fields_ref,
    vel_ref,
    dif_ref,
    ret,
    off_ref,
    obs_ref,
    noise_ref,
    pert_ref,
    bt,
    a2,
    both,
    v_ref,
    w_ref,
    ext,
    velx,
    difx,
    mid,
    own,
    eq,
    vq,
    xs,
    xc,
    yz,
    part,
    rs,
    rowsum,
    rg,
    total,
    m_ref,
    upd,
    local_sem,
    halo_send,
    halo_recv,
    gs_sem,
    gr_sem,
    ss_sem,
    sr_sem,
    zs_sem,
    zr_sem,
):
    g, s = lax.axis_index("grp"), lax.axis_index("slab")
    members, planes, ys, xsz = fields_ref.shape
    units = planes * ys
    per = units // groups
    order = members * groups
    depth = order // (2 * groups)
    last = planes + STEPS

    loads = [
        pltpu.make_async_copy(source, target, local_sem.at[i])
        for i, (source, target) in enumerate(
            (
                (off_hbm, off_ref),
                (noise_hbm, noise_ref),
                (obs_hbm, obs_ref),
                (pert_hbm, pert_ref),
                (fields_ref, ext.at[:, 2:last]),
                (vel_ref, velx.at[:, 1 : planes + 1]),
                (dif_ref, difx.at[1 : planes + 1]),
            )
        )
    ]
    for copy in loads:
        copy.start()

    core, z = lax.rem(s, 2), lax.div(s, 2)
    place, places, heights = g * 2 + core, 2 * groups, slabs // 2

    def plane_peer(r):
        other = lax.rem(place + r, places)
        return other, (lax.div(other, 2), z * 2 + lax.rem(other, 2))

    def height_peer(r):
        return (g, lax.rem(z + r, heights) * 2 + core)

    barrier = pltpu.get_barrier_semaphore()
    for r in range(1, places):
        pl.semaphore_signal(barrier, inc=1, device_id=plane_peer(r)[1], device_id_type=MESH)
    for r in range(1, heights):
        pl.semaphore_signal(barrier, inc=1, device_id=height_peer(r), device_id_type=MESH)
    across = (g, lax.rem(s + 2 * core - 1 + slabs, slabs))
    pl.semaphore_signal(barrier, inc=1, device_id=across, device_id_type=MESH)

    def coefficients(p):
        courant = [velx[c, p].astype(jnp.float32)[None] * COURANT for c in range(3)]
        return courant + [difx[p][None]]

    def first_step(p, carry):
        mid[:, p] = advance(ext[:, p], ext[:, p + 1], ext[:, p + 2], *coefficients(p))
        return carry

    def second_step(p, carry):
        res = advance(mid[:, p], mid[:, p + 1], mid[:, p + 2], *coefficients(p + 1))
        own[pl.ds(p * ys, ys)] = jnp.swapaxes(res, 0, 1)
        return carry

    for copy in loads[4:]:
        copy.wait()
    lax.fori_loop(2, planes, first_step, 0)
    lax.fori_loop(2, planes - 2, second_step, 0)
    pl.semaphore_wait(barrier, places + heights - 1)

    def halo(sign, k, src, dst):
        return pltpu.make_async_remote_copy(
            src_ref=src,
            dst_ref=dst,
            send_sem=halo_send.at[(sign + 1) // 2, k],
            recv_sem=halo_recv.at[(sign + 1) // 2, k],
            device_id=(g, lax.rem(s + sign + slabs, slabs)),
            device_id_type=MESH,
        )

    up = [
        halo(1, 0, fields_ref.at[:, planes - 2 : planes], ext.at[:, 0:2]),
        halo(1, 1, vel_ref.at[:, planes - 1 : planes], velx.at[:, 0:1]),
        halo(1, 2, dif_ref.at[planes - 1 : planes], difx.at[0:1]),
    ]
    down = [
        halo(-1, 0, fields_ref.at[:, 0:2], ext.at[:, last : last + 2]),
        halo(-1, 1, vel_ref.at[:, 0:1], velx.at[:, planes + 1 : planes + 2]),
        halo(-1, 2, dif_ref.at[0:1], difx.at[planes + 1 : planes + 2]),
    ]

    @pl.when(s < slabs - 1)
    def _():
        for copy in up:
            copy.start()

    @pl.when(s > 0)
    def _():
        for copy in down:
            copy.start()

    def grp_copy(phase, r, src, dst):
        return pltpu.make_async_remote_copy(
            src_ref=src,
            dst_ref=dst,
            send_sem=gs_sem.at[phase, r],
            recv_sem=gr_sem.at[phase, r],
            device_id=(lax.rem(g + r, groups), s),
            device_id_type=MESH,
        )

    def plane_copy(phase, r, src, dst):
        return pltpu.make_async_remote_copy(
            src_ref=src,
            dst_ref=dst,
            send_sem=ss_sem.at[phase, r],
            recv_sem=sr_sem.at[phase, r],
            device_id=plane_peer(r)[1],
            device_id_type=MESH,
        )

    def height_copy(r, src, dst):
        return pltpu.make_async_remote_copy(
            src_ref=src,
            dst_ref=dst,
            send_sem=zs_sem.at[r],
            recv_sem=zr_sem.at[r],
            device_id=height_peer(r),
            device_id_type=MESH,
        )

    def units_of(r):
        return pl.ds(lax.rem(g + r, groups) * per, per)

    def inner(r):
        q = lax.rem(g + r, groups)
        return jnp.logical_and(q * per >= 2 * ys, (q + 1) * per <= (planes - 2) * ys)

    e_copies = [grp_copy(1, r, own.at[units_of(r)], eq.at[g]) for r in range(1, groups)]
    for r, copy in enumerate(e_copies):
        pl.when(inner(r + 1))(copy.start)

    loads[0].wait()
    spread_low(bt, off_ref[...])
    for copy in loads[1:4]:
        copy.wait()
    noise = noise_ref[...]
    slot = lax.broadcasted_iota(jnp.int32, noise.shape, 1)
    inverse = jnp.where(slot < count_ref[0], 1.0 / noise, 0.0)
    first, second = split_two((obs_ref[...] / noise + pert_ref[...]) * inverse)
    both[0:members, :] = first
    both[members : 2 * members, :] = second
    off_ref[...] = off_ref[...] // bt.shape[0]

    def v_copy(r):
        return grp_copy(0, r, v_ref.at[units_of(r)], vq.at[g])

    def scatter_turn(r, carry):
        q = lax.rem(g + r, groups)

        def store(u, value):
            v_ref[q * per + u] = value

        scatter_group(q, off_ref, both, bt, a2, store)

        @pl.when(r < groups)
        def _():
            v_copy(r).start()

        return carry

    lax.fori_loop(1, EARLY, scatter_turn, 0)

    @pl.when(s == 0)
    def _():
        ext[:, 0:2] = jnp.zeros((members, 2, ys, xsz), jnp.float32)
        velx[:, 0:1] = jnp.zeros((3, 1, ys, xsz), jnp.int32)
        difx[0:1] = jnp.zeros((1, ys, xsz), jnp.float32)

    @pl.when(s == slabs - 1)
    def _():
        ext[:, last : last + 2] = jnp.zeros((members, 2, ys, xsz), jnp.float32)
        velx[:, planes + 1 : planes + 2] = jnp.zeros((3, 1, ys, xsz), jnp.int32)
        difx[planes + 1 : planes + 2] = jnp.zeros((1, ys, xsz), jnp.float32)

    @pl.when(s > 0)
    def _():
        for copy in up:
            copy.wait_recv()

    @pl.when(s < slabs - 1)
    def _():
        for copy in down:
            copy.wait_recv()

    lax.fori_loop(0, 2, first_step, 0)
    lax.fori_loop(planes, planes + 2, first_step, 0)

    @pl.when(s == 0)
    def _():
        mid[:, 0] = jnp.zeros((members, ys, xsz), jnp.float32)

    @pl.when(s == slabs - 1)
    def _():
        mid[:, planes + 1] = jnp.zeros((members, ys, xsz), jnp.float32)

    lax.fori_loop(0, 2, second_step, 0)
    lax.fori_loop(planes - 2, planes, second_step, 0)
    for r, copy in enumerate(e_copies):
        pl.when(jnp.logical_not(inner(r + 1)))(copy.start)
    eq[g] = own[units_of(0)]
    lax.fori_loop(EARLY, groups + 1, scatter_turn, 0)
    vq[g] = v_ref[units_of(0)]
    scatter_weights(g, per // (bt.shape[0] // LANES), off_ref, inverse * inverse, bt, w_ref)
    v_copies = [v_copy(r) for r in range(1, groups)]
    for copy in v_copies:
        copy.wait_recv()
    for copy in e_copies:
        copy.wait_recv()

    per_row = w_ref.shape[0]
    for u in range(per):
        lanes = slice(u * LANES, (u + 1) * LANES)
        x = jnp.concatenate([eq[q, u] for q in range(groups)], axis=0)
        v = jnp.concatenate([vq[q, u] for q in range(groups)], axis=0)
        w = w_ref[u % per_row, u // per_row : u // per_row + 1, :]
        centered = x - jnp.sum(x, axis=0, keepdims=True) / order
        xs[:, lanes] = x
        first, second = split_two(centered)
        high, low = split_two(jnp.concatenate([centered * w, v - x * w], axis=0))
        for t, (left, right) in enumerate(((first, high), (first, low), (second, high))):
            at = (t * per + u) * LANES
            xc[:, at : at + LANES] = left.astype(jnp.bfloat16)
            yz[:, at : at + LANES] = right.astype(jnp.bfloat16)
    part[...] = lax.dot_general(
        xc[...],
        yz[...],
        NT,
        preferred_element_type=jnp.float32,
    ) / (order - 1)

    def rows_of(block):
        return pl.ds(pl.multiple_of(block * depth, depth), depth)

    rs_copies = [
        plane_copy(0, r, part.at[rows_of(plane_peer(r)[0])], rs.at[place])
        for r in range(1, places)
    ]
    for copy in rs_copies:
        copy.start()
    rs[place] = part[rows_of(place), :]
    for copy in rs_copies:
        copy.wait_recv()
    added = rs[0]
    for i in range(1, places):
        added = added + rs[i]
    rowsum[...] = added
    rg_copies = [height_copy(r, rowsum, rg.at[z]) for r in range(1, heights)]
    for copy in rg_copies:
        copy.start()
    rg[z] = added
    for copy in rg_copies:
        copy.wait_recv()
    added = rg[0]
    for i in range(1, heights):
        added = added + rg[i]
    total[...] = added
    ag_copies = [plane_copy(1, r, total, m_ref.at[rows_of(place)]) for r in range(1, places)]
    for copy in ag_copies:
        copy.start()
    m_ref[rows_of(place), :] = added
    for copy in ag_copies:
        copy.wait_recv()

    shape = m_ref.shape
    diagonal = lax.broadcasted_iota(jnp.int32, shape, 0) == lax.broadcasted_iota(
        jnp.int32, shape, 1
    )
    m_ref[...] = m_ref[...] + jnp.where(diagonal, 1.0, 0.0)
    solve_in_place(m_ref)

    new = xs[...] + lax.dot_general(
        m_ref[:, 0:order],
        xs[...],
        TN,
        precision=lax.Precision.HIGHEST,
        preferred_element_type=jnp.float32,
    )
    for q in range(groups):
        for u in range(per):
            upd[q, u] = new[q * members : (q + 1) * members, u * LANES : (u + 1) * LANES]
    u_copies = [
        grp_copy(2, r, upd.at[lax.rem(g + r, groups)], ret.at[units_of(0)])
        for r in range(1, groups)
    ]
    for copy in u_copies:
        copy.start()
    ret[units_of(0)] = upd[g]
    for copy in u_copies:
        copy.wait_recv()

    for copy in v_copies + e_copies + rs_copies + rg_copies + ag_copies + u_copies:
        copy.wait_send()

    @pl.when(s < slabs - 1)
    def _():
        for copy in up:
            copy.wait_send()

    @pl.when(s > 0)
    def _():
        for copy in down:
            copy.wait_send()


def finish_kernel(ret, out_hbm, stage, sem):
    planes = out_hbm.shape[1]
    ys = out_hbm.shape[2]
    copies = []
    for p in range(planes):
        stage[p] = jnp.swapaxes(ret[p * ys : (p + 1) * ys], 0, 1)
        copies.append(pltpu.make_async_copy(stage.at[p], out_hbm.at[:, p], sem.at[p]))
        copies[-1].start()
    for copy in copies:
        copy.wait()


def local(
    groups,
    slabs,
    fields,
    velocity,
    diffusivity,
    sensor_offsets,
    sensor_counts,
    observations,
    noise_scale,
    perturbation,
):
    members, planes, ys, xsz = fields.shape
    units = planes * ys
    per = units // groups
    order = members * groups
    depth = order // (2 * groups)
    slots = sensor_offsets.shape[0]
    width = 2 * LANES
    per_group = per * LANES // width
    vmem = pl.BlockSpec(memory_space=pltpu.VMEM)
    f32 = jnp.float32
    scratch = [
        pltpu.VMEM((1, slots), jnp.int32),
        pltpu.VMEM((1, slots), f32),
        pltpu.VMEM((1, slots), f32),
        pltpu.VMEM((members, slots), f32),
        pltpu.VMEM((width, slots), jnp.bfloat16),
        pltpu.VMEM((per_group * 2 * members, slots), jnp.bfloat16),
        pltpu.VMEM((2 * members, slots), f32),
        pltpu.VMEM((units, members, xsz), f32),
        pltpu.VMEM((width // LANES, -(-per_group // 8) * 8, LANES), f32),
        pltpu.VMEM((members, planes + 4, ys, xsz), f32),
        pltpu.VMEM((3, planes + 2, ys, xsz), jnp.int32),
        pltpu.VMEM((planes + 2, ys, xsz), f32),
        pltpu.VMEM((members, planes + 2, ys, xsz), f32),
        pltpu.VMEM((units, members, xsz), f32),
        pltpu.VMEM((groups, per, members, xsz), f32),
        pltpu.VMEM((groups, per, members, xsz), f32),
        pltpu.VMEM((order, per * xsz), f32),
        pltpu.VMEM((order, 3 * per * xsz), jnp.bfloat16),
        pltpu.VMEM((2 * order, 3 * per * xsz), jnp.bfloat16),
        pltpu.VMEM((order, 2 * order), f32),
        pltpu.VMEM((2 * groups, depth, 2 * order), f32),
        pltpu.VMEM((depth, 2 * order), f32),
        pltpu.VMEM((slabs // 2, depth, 2 * order), f32),
        pltpu.VMEM((depth, 2 * order), f32),
        pltpu.VMEM((order, 2 * order), f32),
        pltpu.VMEM((groups, per, members, xsz), f32),
        pltpu.SemaphoreType.DMA((7,)),
        pltpu.SemaphoreType.DMA((2, 3)),
        pltpu.SemaphoreType.DMA((2, 3)),
        pltpu.SemaphoreType.DMA((3, groups)),
        pltpu.SemaphoreType.DMA((3, groups)),
        pltpu.SemaphoreType.DMA((2, 2 * groups)),
        pltpu.SemaphoreType.DMA((2, 2 * groups)),
        pltpu.SemaphoreType.DMA((slabs // 2,)),
        pltpu.SemaphoreType.DMA((slabs // 2,)),
    ]
    anywhere = pl.BlockSpec(memory_space=pl.ANY)
    ret = pl.pallas_call(
        functools.partial(step_kernel, groups, slabs),
        out_shape=jax.ShapeDtypeStruct((units, members, xsz), f32),
        in_specs=[pl.BlockSpec(memory_space=pltpu.SMEM)] + [anywhere] * 7,
        out_specs=vmem,
        scratch_shapes=scratch,
        compiler_params=pltpu.CompilerParams(
            collective_id=0, has_side_effects=True, vmem_limit_bytes=56 * 1024 * 1024
        ),
        name="ensemble_step",
    )(
        sensor_counts,
        sensor_offsets[None],
        observations[None],
        noise_scale[None],
        perturbation,
        fields,
        velocity,
        diffusivity,
    )
    return pl.pallas_call(
        finish_kernel,
        out_shape=jax.ShapeDtypeStruct(fields.shape, f32),
        in_specs=[vmem],
        out_specs=anywhere,
        scratch_shapes=[
            pltpu.VMEM((planes, members, ys, xsz), f32),
            pltpu.SemaphoreType.DMA((planes,)),
        ],
        name="finish",
    )(ret)


def solution(mesh):
    return jax.shard_map(
        functools.partial(local, mesh.shape["grp"], mesh.shape["slab"]),
        mesh=mesh,
        in_specs=(
            P("grp", "slab", None, None),
            P(None, "slab", None, None),
            P("slab", None, None),
            P("slab"),
            P("slab"),
            P("slab"),
            P("slab"),
            P("grp", "slab"),
        ),
        out_specs=P("grp", "slab", None, None),
        check_vma=False,
    )
```
